128 devices in a mesh: sec: 4 (over y), dp: 8 (over x_hi, z), mp: 4 (over x_lo, core).
Axes of the slice: x: 4 (x_hi: 2, x_lo: 2; x = x_hi * 2 + x_lo), y: 4, z: 4, core: 2. Of those that a mesh axis runs over, the one named last changes fastest.
Arguments:
- patches: bfloat16 [320, 5120], P('dp'), may hold values from -6 to 6
- ln_gain: bfloat16 [1280], replicated, may hold values from 0.099609375 to 1.8984375
- ln_shift: bfloat16 [1280], replicated, may hold values from -3 to 3
- w_in: bfloat16 [5120, 5120], P('dp', ('sec', 'mp')), may hold values from -0.078125 to 0.078125
- b_in: bfloat16 [5120], P(('sec', 'mp')), may hold values from -3 to 3
- w_out: bfloat16 [5120, 8192], P(('sec', 'mp'), 'dp'), may hold values from -0.125 to 0.125
- b_out: bfloat16 [8192], P(('sec', 'mp')), may hold values from -3 to 3
- place: int32 [320], P('dp'), may hold values from 0 to 255, as said below
- image_counts: int32 [8], P('dp'), may hold values from 1 to 40, 128 in all
- text_rows: bfloat16 [2048, 8192], P('dp', ('sec', 'mp')), may hold values from -6 to 6
- segments: int32 [8, 256], P('dp'), may hold values from 0 to 3, never falling along the last dimension, each value on 1 to 128 neighbouring positions
- norm_gain: bfloat16 [2, 8192], replicated, may hold values from 0.099609375 to 1.8984375
- q_weight: bfloat16 [2, 8192, 4096], P(None, None, ('sec', 'mp'))
- kv_weight: bfloat16 [2, 2, 512, 8192], P(None, None, ('sec', 'mp'))
- o_weight: bfloat16 [2, 4096, 8192], P(None, ('sec', 'mp')), may hold values from -0.125 to 0.125
- grad_rows: bfloat16 [320, 8192], P('dp'), may hold values from -6 to 6
Outputs:
- final_rows: float32 [2048, 8192], P('dp', ('sec', 'mp'))
- patch_grads: float32 [320, 5120], P('dp')
The draws below stay inside these ranges and needn't reach their ends.
Inputs may be any that keep to these rules, and one draw needn't show every extreme that they name: `place`: each owner's 40 entries are distinct token positions of its own packed sequence; only an owner's first image_counts entries are used. `image_counts`: the counts sum to 8 * (16) over all owners.
All inputs are finite; a program needn't handle non-finite values. No bound on the sum of `image_counts` on one device may be relied on, other than what follows from the above.
Results may differ from the reference program's by a relative error of at most 0.0055.
Values may be sent and summed in bfloat16 or wider, within the bound.
A program may use at most 128 MiB of HBM per device.

```python
import math
import jax
import jax.numpy as jnp
import numpy as np
from jax import lax

D = 8192
HEADS = 32
KV_HEADS = 4
HEAD_DIM = 128
VIT = 1280
MHID = 5120
LAYERS = 2
DOCS = 4
TOK = 256
MERGE_IN = 5120
CAP = 40
SLOTS = 320
TOKENS = 2048
N_SEC = 4
N_DP = 8
N_MP = 4


def attention_tables(key):
    base = jax.random.fold_in(key, 11)
    key_query, key_keys, key_values = jax.random.split(base, 3)
    fan_scale = D ** (-0.5)
    key_table = jax.random.normal(key_keys, (LAYERS, KV_HEADS * HEAD_DIM, D), jnp.float32) * fan_scale
    value_table = jax.random.normal(key_values, (LAYERS, KV_HEADS * HEAD_DIM, D), jnp.float32) * fan_scale
    query_table = jax.random.normal(key_query, (LAYERS, D, HEADS, HEAD_DIM), jnp.float32) * fan_scale
    return (query_table.reshape(LAYERS, D, HEADS * HEAD_DIM), jnp.stack([key_table, value_table], axis=1))


def draw_q_weight(key, part):
    return attention_tables(key)[0].astype(jnp.bfloat16)


def draw_kv_weight(key, part):
    return attention_tables(key)[1].astype(jnp.bfloat16)


def draw_place(key, part):
    owner_keys = jax.random.split(jax.random.fold_in(key, 23), N_DP)

    def one_owner(owner_key):
        inner = jax.random.permutation(owner_key, TOK - 2)[:CAP - 2] + 1
        edges = jnp.array([0, TOK - 1], dtype=jnp.int32)
        listed = jnp.concatenate([edges, inner.astype(jnp.int32)])
        return jax.random.permutation(jax.random.fold_in(owner_key, 5), listed)
    return jax.vmap(one_owner)(owner_keys).reshape(N_DP * CAP).astype(jnp.int32)


def spiked(values, rng, source, target, blocks, factor):
    def block_of(position):
        return (jnp.arange(values.shape[position]) // (values.shape[position] // blocks)).reshape((-1,) + (1,) * (values.ndim - 1 - position))

    near = jax.random.permutation(rng, blocks)[block_of(target)]
    second = (block_of(target) + blocks // 2) % blocks
    return jnp.where((block_of(source) == near) | (block_of(source) == second), factor * values, values)


def block_levels(key, shape, shards, low, largest):
    level = 1.0
    for position, parts in shards:
        steps = jax.random.uniform(jax.random.fold_in(jax.random.fold_in(key, 6), position), (parts,), jnp.float32, low / len(shards), largest / len(shards))
        level = level * jnp.repeat(jnp.exp(steps), shape[position] // parts).reshape((-1,) + (1,) * (len(shape) - 1 - position))
    return level


def profile(count, total, most, skew):
    portions = [(1 << 20) // math.isqrt(standing ** skew) + 1 for standing in range(2, count + 1)]
    surplus, given = total - most - (count - 1), [1] * (count - 1)
    while surplus > 0:
        candidates = [i for i in range(count - 1) if given[i] < most]
        pool, budget = sum([portions[i] for i in candidates]), surplus
        for i in candidates:
            extra = min(most - given[i], max(1, budget * portions[i] // pool), surplus)
            given[i] = given[i] + extra
            surplus = surplus - extra
    return np.array([most] + given)


def uneven_parts(key, number_of, total, limit, lean):
    if number_of == 2:
        one = jax.random.randint(key, (), max(1, total - limit), min(limit, total - 1) + 1)
        return jnp.stack([one, total - one])
    sizes = jnp.asarray(profile(number_of, total, limit, lean), jnp.int32)
    pairs = (number_of - 1) // 2
    donor, receiver = sizes[1:1 + 2 * pairs:2], sizes[2:2 + 2 * pairs:2]
    margin = jnp.minimum(donor - 1, limit - receiver)
    shifted = jax.random.randint(jax.random.fold_in(key, 1), (pairs,), 0, 1 << 20) % (margin + 1)
    sizes = sizes.at[1:1 + 2 * pairs:2].set(donor - shifted).at[2:2 + 2 * pairs:2].set(receiver + shifted)
    return sizes[jax.random.permutation(jax.random.fold_in(key, 2), number_of)]


def scatter_about(rng, shape, scale, most, cuts=(), kind=jnp.bfloat16):
    loudness = block_levels(rng, shape, cuts, -0.22, 0.18) if cuts else 1.0
    entries = jax.random.normal(rng, shape, jnp.float32) * scale * loudness
    return jnp.minimum(jnp.maximum(entries, -most), most).astype(kind)


def noise_with(own_key, shape, scale, reach, shards, heavy, kind=jnp.bfloat16):
    result = scale * jax.random.normal(own_key, shape, jnp.float32)
    if shards:
        result = result * block_levels(own_key, shape, shards, -0.22, 0.18)
    return jnp.clip(spiked(result, jax.random.fold_in(own_key, 3), *heavy), -reach, reach).astype(kind)


def setup_inputs(seed: int = 0) -> dict:
    streams_of = jax.random.split(jax.random.key(seed), 17)
    return {
        "patches": scatter_about(streams_of[0], (SLOTS, MERGE_IN), 1.0, 6.0, ((0, 8),)),
        "ln_gain": jnp.clip(1.0 + 0.18 * jax.random.normal(streams_of[1], (VIT,), jnp.float32), 0.099609375, 1.8984375).astype(jnp.bfloat16),
        "ln_shift": scatter_about(streams_of[2], (VIT,), 0.5, 3.0),
        "w_in": scatter_about(streams_of[3], (MERGE_IN, MHID), MERGE_IN ** -0.5, 0.078125, ((0, 8), (1, 16))),
        "b_in": scatter_about(streams_of[4], (MHID,), 0.5, 3.0, ((0, 16),)),
        "w_out": noise_with(streams_of[5], (MHID, D), MHID ** -0.5, 0.125, ((0, 16), (1, 8)), (0, 1, 16, 2.0)),
        "b_out": scatter_about(streams_of[6], (D,), 0.5, 3.0, ((0, 16),)),
        "place": draw_place(jax.random.fold_in(streams_of[16], 71), 0),
        "image_counts": uneven_parts(streams_of[8], N_DP, N_DP * (TOK // 16), CAP, 2).astype(jnp.int32),
        "text_rows": scatter_about(streams_of[9], (TOKENS, D), 1.0, 6.0, ((0, 8), (1, 16))),
        "segments": jax.vmap(lambda own: jnp.searchsorted(jnp.cumsum(uneven_parts(own, DOCS, TOK, TOK // 2, 1)), jnp.arange(TOK), side="right"))(jax.random.split(streams_of[10], N_DP)).reshape((N_DP, TOK)).astype(jnp.int32),
        "norm_gain": jnp.clip(1.0 + 0.18 * jax.random.normal(streams_of[11], (LAYERS, D), jnp.float32), 0.099609375, 1.8984375).astype(jnp.bfloat16),
        "q_weight": draw_q_weight(jax.random.fold_in(streams_of[16], 71), 0),
        "kv_weight": draw_kv_weight(jax.random.fold_in(streams_of[16], 71), 0),
        "o_weight": noise_with(streams_of[14], (LAYERS, HEADS * HEAD_DIM, D), (HEADS * HEAD_DIM) ** -0.5, 0.125, ((1, 16),), (1, 2, 16, 2.0)),
        "grad_rows": scatter_about(streams_of[15], (SLOTS, D), 1.0, 6.0, ((0, 8),)),
    }


ln_eps = 1e-06
rms_eps = 1e-06
rope_base = 1000000.0

def group_norm(patch_rows, ln_gain, ln_shift):
    row_count = patch_rows.shape[0]
    grouped = patch_rows.astype(jnp.float32).reshape(row_count, -1, ln_gain.shape[0])
    center = grouped - lax.optimization_barrier(jnp.mean(grouped, axis=-1, keepdims=True))
    spread = lax.optimization_barrier(jnp.mean(center * center, axis=-1, keepdims=True))
    scaled = center * lax.rsqrt(spread + ln_eps) * ln_gain.astype(jnp.float32) + ln_shift.astype(jnp.float32)
    return scaled.reshape(row_count, -1)

def gelu_exact(values):
    return jax.nn.gelu(values, approximate=False)

def rotate(values, positions):
    head_depth = values.shape[-1]
    half_depth = head_depth // 2
    inv_freq = rope_base ** (-2.0 * jnp.arange(half_depth, dtype=jnp.float32) / head_depth)
    angles = positions[:, None] * inv_freq[None, :]
    cosine = jnp.cos(angles)[:, None, :]
    sine_part = jnp.sin(angles)[:, None, :]
    first_half = values[..., :half_depth]
    second = values[..., half_depth:]
    return jnp.concatenate([first_half * cosine - second * sine_part, second * cosine + first_half * sine_part], axis=-1)

def doc_mask(segment_ids):
    token_index = jnp.arange(segment_ids.shape[0], dtype=jnp.int32)
    same_doc = segment_ids[:, None] == segment_ids[None, :]
    allowed = same_doc & (token_index[None, :] <= token_index[:, None])
    positions = lax.optimization_barrier(jnp.sum(allowed.astype(jnp.int32), axis=1)) - 1
    return (allowed, positions.astype(jnp.float32))

def rms_rows(hidden, gain_row):
    values = hidden.astype(jnp.float32)
    factor = lax.rsqrt(lax.optimization_barrier(jnp.mean(values * values, axis=-1, keepdims=True)) + rms_eps)
    return (values * factor * gain_row.astype(jnp.float32)).astype(jnp.bfloat16)

def section(hidden, allowed, positions, gain_row, q_layer, kv_layer, o_layer):
    token_count = hidden.shape[0]
    normed = rms_rows(hidden, gain_row)
    queries = jnp.dot(normed, q_layer, preferred_element_type=jnp.float32).reshape(token_count, HEADS, HEAD_DIM)
    key_rows = lax.dot_general(normed, kv_layer[0], (((1,), (1,)), ((), ())), preferred_element_type=jnp.float32)
    value_rows = lax.dot_general(normed, kv_layer[1], (((1,), (1,)), ((), ())), preferred_element_type=jnp.float32)
    key_rows = key_rows.reshape(token_count, KV_HEADS, HEAD_DIM)
    value_rows = value_rows.reshape(token_count, KV_HEADS, HEAD_DIM)
    queries = rotate(queries, positions).astype(jnp.bfloat16)
    key_rows = rotate(key_rows, positions).astype(jnp.bfloat16)
    value_rows = value_rows.astype(jnp.bfloat16)
    group_size = HEADS // KV_HEADS
    key_heads = jnp.repeat(key_rows, group_size, axis=1)
    value_heads = jnp.repeat(value_rows, group_size, axis=1)
    scores = jnp.einsum('thd,shd->hts', queries.astype(jnp.float32), key_heads.astype(jnp.float32)) * (1.0 / math.sqrt(HEAD_DIM))
    scores = jnp.where(allowed[None], scores, -jnp.inf)
    row_max = lax.optimization_barrier(jnp.max(scores, axis=-1, keepdims=True))
    exp_scores = jnp.exp(scores - row_max)
    attn_weights = (exp_scores / lax.optimization_barrier(jnp.sum(exp_scores, axis=-1, keepdims=True))).astype(jnp.bfloat16)
    attended = jnp.einsum('hts,shd->thd', attn_weights.astype(jnp.float32), value_heads.astype(jnp.float32)).astype(jnp.bfloat16)
    group_count = N_SEC * N_MP
    attended = attended.reshape(token_count, group_count, -1)
    o_groups = o_layer.reshape(group_count, -1, D)
    group_terms = jnp.einsum('tgc,gcd->gtd', attended.astype(jnp.float32), o_groups.astype(jnp.float32))
    return hidden.astype(jnp.float32) + lax.optimization_barrier(jnp.sum(group_terms, axis=0))

def reference(patches, ln_gain, ln_shift, w_in, b_in, w_out, b_out, place, image_counts, text_rows, segments, norm_gain, q_weight, kv_weight, o_weight, grad_rows):
    normed = group_norm(patches, ln_gain, ln_shift).astype(jnp.bfloat16)
    pre_act = jnp.dot(normed, w_in, preferred_element_type=jnp.float32) + b_in.astype(jnp.float32)
    hidden_units = gelu_exact(pre_act).astype(jnp.bfloat16)
    merged = (jnp.dot(hidden_units, w_out, preferred_element_type=jnp.float32) + b_out.astype(jnp.float32)).astype(jnp.bfloat16)
    slot_index = jnp.arange(CAP, dtype=jnp.int32)
    token_index = jnp.arange(TOK, dtype=jnp.int32)
    live_slot = slot_index[None, :] < image_counts[:, None]
    select = (place.reshape(N_DP, CAP)[:, :, None] == token_index[None, None, :]) & live_slot[:, :, None]
    is_image = jnp.any(select, axis=1)
    picked = jnp.einsum('oct,ocd->otd', select.astype(jnp.float32), merged.reshape(N_DP, CAP, D).astype(jnp.float32))
    start_rows = jnp.where(is_image[:, :, None], picked, text_rows.reshape(N_DP, TOK, D).astype(jnp.float32)).astype(jnp.bfloat16)

    def run_owner(owner_args):
        current, segment_ids = owner_args
        current = current.astype(jnp.float32)
        allowed, positions = doc_mask(segment_ids)
        for layer_index in range(LAYERS):
            current = section(current, allowed, positions, norm_gain[layer_index], q_weight[layer_index], kv_weight[layer_index], o_weight[layer_index])
        return current
    final_rows = lax.map(run_owner, (start_rows, segments)).reshape(N_DP * TOK, D)
    slot_grads = jnp.where(live_slot.reshape(N_DP * CAP)[:, None], grad_rows, jnp.zeros_like(grad_rows))
    hidden_grads = lax.dot_general(slot_grads, w_out, (((1,), (1,)), ((), ())), preferred_element_type=jnp.float32)
    _, pull_gelu = jax.vjp(gelu_exact, pre_act)
    pre_grads = pull_gelu(hidden_grads)[0].astype(jnp.bfloat16)
    normed_grads = lax.dot_general(pre_grads, w_in, (((1,), (1,)), ((), ())), preferred_element_type=jnp.float32)
    _, pull_norm = jax.vjp(lambda values: group_norm(values, ln_gain, ln_shift), patches.astype(jnp.float32))
    patch_grads = pull_norm(normed_grads)[0]
    return (final_rows, patch_grads)
```

```python
import functools
import math

import jax
import jax.numpy as jnp
from jax import lax
from jax.experimental import pallas as pl
from jax.experimental.pallas import tpu as pltpu
from jax.sharding import PartitionSpec as P

D = 8192
HEAD_DIM = 128
PAD = 48

ln_eps = 1e-06
rms_eps = 1e-06
rope_base = 1000000.0

MESH = pl.DeviceIdType.MESH
F32 = jnp.float32
BF16 = jnp.bfloat16


class Place:
    def __init__(self):
        self.y = lax.axis_index("sec")
        self.d = lax.axis_index("dp")
        mp = lax.axis_index("mp")
        self.mp = mp
        self.x = mp // 2
        self.c = lax.rem(mp, 2)
        self.yu = lax.rem(self.y + 1, 4)
        self.yd = lax.rem(self.y + 3, 4)
        self.ya = lax.rem(self.y + 2, 4)
        self.xo = 1 - self.x
        self.co = 1 - self.c
        self.U = self.dev(self.yu, self.x, self.c)
        self.Dn = self.dev(self.yd, self.x, self.c)
        self.X = self.dev(self.y, self.xo, self.c)
        self.C = self.dev(self.y, self.x, self.co)
        self.XC = self.dev(self.y, self.xo, self.co)
        self.me = self.sid(self.y, self.x, self.c)

    def dev(self, y, x, c):
        return {"sec": y, "dp": self.d, "mp": x * 2 + c}

    def sid(self, y, x, c):
        return y * 4 + x * 2 + c


def rcopy(src, dst, ssem, rsem, dev):
    return pltpu.make_async_remote_copy(
        src_ref=src, dst_ref=dst, send_sem=ssem, recv_sem=rsem, device_id=dev, device_id_type=MESH
    )


def barrier_with(devs):
    sem = pltpu.get_barrier_semaphore()
    for dev in devs:
        pl.semaphore_signal(sem, inc=1, device_id=dev, device_id_type=MESH)
    pl.semaphore_wait(sem, len(devs))


class Gather:
    def __init__(self, pl_, buf, rows, ssem, rsem):
        self.p, self.buf, self.half = pl_, buf, rows // 2
        self.ssem, self.rsem = ssem, rsem
        self.sent = []

    def view(self, s, h):
        return self.buf.at[s, pl.ds(h * self.half, self.half), :]

    def send(self, s, h, dev):
        k = len(self.sent)
        cp = rcopy(self.view(s, h), self.view(s, h), self.ssem.at[k], self.rsem.at[s * 2 + h], dev)
        cp.start()
        self.sent.append(cp)

    def wait(self, s, h):
        rcopy(
            self.view(s, h), self.view(s, h), self.ssem.at[0], self.rsem.at[s * 2 + h], self.p.C
        ).wait_recv()

    def wait_all(self, s):
        self.wait(s, 0)
        self.wait(s, 1)

    def start(self):
        p = self.p
        for h in range(2):
            for dev in (p.X, p.U, p.Dn, p.C):
                self.send(p.me, h, dev)

    def first(self):
        p = self.p
        for h in range(2):
            s = p.sid(p.y, p.xo, p.c)
            self.wait(s, h)
            self.send(s, h, p.U)
            self.send(s, h, p.Dn)
            self.send(s, h, p.C)
            s = p.sid(p.yd, p.x, p.c)
            self.wait(s, h)
            if h == 0:
                self.send(s, h, p.U)
            self.send(s, h, p.C)
            s = p.sid(p.yu, p.x, p.c)
            self.wait(s, h)
            if h == 1:
                self.send(s, h, p.Dn)
            self.send(s, h, p.C)

    def second(self):
        p = self.p
        s = p.sid(p.ya, p.x, p.c)
        for h in range(2):
            self.wait(s, h)
            self.send(s, h, p.X)
            self.send(s, h, p.C)
        for h in range(2):
            for y in (p.yd, p.yu):
                s = p.sid(y, p.xo, p.c)
                self.wait(s, h)
                self.send(s, h, p.C)

    def third(self):
        p = self.p
        s = p.sid(p.ya, p.xo, p.c)
        for h in range(2):
            self.wait(s, h)
            self.send(s, h, p.C)

    def drain(self):
        for cp in self.sent:
            cp.wait_send()


GATHER_SENDS = 30


class Scatter:
    def __init__(self, pl_, sb, rb, parts, ssem, rsem, piece):
        self.p, self.sb, self.rb, self.parts = pl_, sb, rb, parts
        self.ssem, self.rsem, self.piece = ssem, rsem, piece
        self.sent = []

    def copy(self, i, part, dev):
        return rcopy(
            self.sb.at[i].at[self.parts[part]],
            self.rb.at[i].at[self.parts[part]],
            self.ssem.at[i * 2 + part],
            self.rsem.at[i * 2 + part],
            dev,
        )

    def send(self, i, part, dev, value):
        self.sb.at[i][self.parts[part]] = value.astype(BF16)
        cp = self.copy(i, part, dev)
        cp.start()
        self.sent.append(cp)

    def got(self, i, part):
        self.copy(i, part, self.p.C).wait_recv()
        return self.rb.at[i][self.parts[part]].astype(F32)

    def first(self, part):
        p, piece = self.p, self.piece
        self.send(0, part, p.X, piece(p.ya, p.xo, part))
        self.send(1, part, p.U, piece(p.yu, p.xo, part))
        self.send(2, part, p.Dn, piece(p.yd, p.xo, part))
        if part == 1:
            self.send(5, 1, p.U, piece(p.yu, p.x, 1))
        else:
            self.send(6, 0, p.Dn, piece(p.yd, p.x, 0))

    def second(self, part):
        p, piece = self.p, self.piece
        own = piece(p.ya, p.x, part)
        self.send(3, part, p.U if part == 0 else p.Dn, own + self.got(0, part))
        own = piece(p.y, p.xo, part)
        self.send(4, part, p.X, own + self.got(1, part) + self.got(2, part))

    def third(self):
        p, piece = self.p, self.piece
        own = piece(p.yu, p.x, 0)
        self.send(5, 0, p.U, own + self.got(3, 0))
        own = piece(p.yd, p.x, 1)
        self.send(6, 1, p.Dn, own + self.got(3, 1))

    def last(self, part):
        p = self.p
        own = self.piece(p.y, p.x, part)
        return own + self.got(4, part) + self.got(5, part) + self.got(6, part)

    def drain(self):
        for cp in self.sent:
            cp.wait_send()


def norm_parts(group):
    center = group - jnp.mean(group, axis=-1, keepdims=True)
    spread = jnp.mean(center * center, axis=-1, keepdims=True)
    rstd = lax.rsqrt(spread + ln_eps)
    return center * rstd, rstd


def merger_kernel(
    count_ref,
    patches_ref,
    grads_ref,
    gain_ref,
    shift_ref,
    w_in_ref,
    b_in_ref,
    w_out_ref,
    b_out_ref,
    place_ref,
    text_ref,
    start_ref,
    pg_ref,
    xs,
    gs,
    xall,
    gall,
    psend,
    precv,
    hall,
    csend,
    crecv,
    pieces,
    sb,
    rb,
    fin,
    finr,
    gg,
    sx,
    rx,
    rg,
    sf,
    sp,
    rp,
    sh,
    rh,
    sc,
    rc,
    srs,
    rrs,
    sperm,
    rperm,
    sag,
    rag,
):
    p = Place()
    n_dp = xall.shape[0]
    rows = patches_ref.shape[0]
    vit = gain_ref.shape[1]
    groups = patches_ref.shape[1] // vit
    xw = xall.shape[2]
    gw = gall.shape[2]
    hid = w_in_ref.shape[1]
    half_out = gw // 2
    half_in = xw // 2
    fill = jnp.zeros((PAD - rows, 1), F32)

    def peer(k):
        d = lax.rem(p.d + k, n_dp)
        return d, {"sec": p.y, "dp": d, "mp": p.mp}

    s = p.me
    swap_dp = s // 2
    swap_s = 2 * p.d + lax.rem(s, 2)
    swap = {"sec": swap_s // 4, "dp": swap_dp, "mp": lax.rem(swap_s, 4)}
    stays = jnp.logical_and(swap_dp == p.d, swap_s == s)

    sem = pltpu.get_barrier_semaphore()
    for k in range(1, n_dp):
        pl.semaphore_signal(sem, inc=1, device_id=peer(k)[1], device_id_type=MESH)
    for dev in (p.U, p.Dn, p.X, p.C, swap):
        pl.semaphore_signal(sem, inc=1, device_id=dev, device_id_type=MESH)

    gain = gain_ref[...]
    shift = shift_ref[...]
    for g in range(groups):
        cols = slice(g * vit, (g + 1) * vit)
        unit, _ = norm_parts(patches_ref[:, cols].astype(F32))
        scaled = unit * gain + shift
        xs[:, cols] = jnp.concatenate([scaled, jnp.broadcast_to(fill, (PAD - rows, vit))], 0).astype(
            BF16
        )
    live = lax.broadcasted_iota(jnp.int32, (rows, 1), 0) < count_ref[0]
    step = 1024
    for at in range(0, grads_ref.shape[1], step):
        g = jnp.where(live, grads_ref[:, at : at + step].astype(F32), 0.0)
        gs[:, at : at + step] = jnp.concatenate(
            [g, jnp.broadcast_to(fill, (PAD - rows, step))], 0
        ).astype(BF16)
    pl.semaphore_wait(sem, n_dp - 1 + 5)

    def xcopy(k):
        d, dev = peer(k)
        src = xs.at[:, pl.ds(pl.multiple_of(d * xw, 128), xw)]
        return rcopy(src, xall.at[p.d], sx.at[k], rx.at[p.d], dev)

    def gcopy(k):
        d, dev = peer(k)
        src = gs.at[:, pl.ds(pl.multiple_of(d * gw, 128), gw)]
        return rcopy(src, gall.at[p.d], sx.at[k], rg.at[p.d], dev)

    def xfwd(k):
        d, _ = peer(k)
        return rcopy(xall.at[d], xall.at[d], sf.at[k], rx.at[d], p.C)

    def gfwd(k):
        d, _ = peer(k)
        return rcopy(gall.at[d], gall.at[d], sf.at[k], rg.at[d], p.C)

    ks = list(range(1, n_dp))

    @pl.when(p.c == 0)
    def _():
        for k in ks:
            xcopy(k).start()

    @pl.when(p.c == 1)
    def _():
        for k in ks:
            gcopy(k).start()

    xall[p.d] = xs[:, pl.ds(pl.multiple_of(p.d * xw, 128), xw)]
    gall[p.d] = gs[:, pl.ds(pl.multiple_of(p.d * gw, 128), gw)]

    @pl.when(p.c == 0)
    def _():
        for k in ks:
            xfwd(k).wait_recv()
            xfwd(k).start()
        for k in ks:
            gfwd(k).wait_recv()
        for k in ks:
            xcopy(k).wait_send()
            xfwd(k).wait_send()

    @pl.when(p.c == 1)
    def _():
        for k in ks:
            gfwd(k).wait_recv()
            gfwd(k).start()
        for k in ks:
            xfwd(k).wait_recv()
        for k in ks:
            gcopy(k).wait_send()
            gfwd(k).wait_send()

    flat = n_dp * PAD
    pf = jnp.dot(xall[...].reshape(flat, xw), w_in_ref[...], preferred_element_type=F32)
    psend[:, 0:PAD, :] = pf.astype(BF16).reshape(n_dp, PAD, hid)
    ph = lax.dot_general(
        gall[...].reshape(flat, gw),
        w_out_ref[...],
        (((1,), (1,)), ((), ())),
        preferred_element_type=F32,
    )
    psend[:, PAD:, :] = ph.astype(BF16).reshape(n_dp, PAD, hid)

    def pcopy(k):
        d, dev = peer(k)
        return rcopy(psend.at[d], precv.at[p.d], sp.at[k], rp.at[p.d], dev)

    def pwait(k):
        d, dev = peer(k)
        return rcopy(psend.at[d], precv.at[d], sp.at[k], rp.at[d], dev)

    for k in ks:
        pcopy(k).start()
    total = psend[p.d].astype(F32)
    for k in ks:
        pwait(k).wait_recv()
        total = total + precv[peer(k)[0]].astype(F32)
    for k in ks:
        pcopy(k).wait_send()

    pre_act = total[0:PAD] + b_in_ref[...]
    hidden_grads = total[PAD:]
    cdf = 0.5 * (1.0 + lax.erf(pre_act * (1.0 / math.sqrt(2.0))))
    pdf = jnp.exp(-0.5 * pre_act * pre_act) * (1.0 / math.sqrt(2.0 * math.pi))
    hall[p.d] = jnp.concatenate(
        [pre_act * cdf, hidden_grads * (cdf + pre_act * pdf)], axis=0
    ).astype(BF16)

    def hcopy(k):
        _, dev = peer(k)
        return rcopy(hall.at[p.d], hall.at[p.d], sh.at[k], rh.at[p.d], dev)

    def hwait(k):
        d, dev = peer(k)
        return rcopy(hall.at[d], hall.at[d], sh.at[k], rh.at[d], dev)

    for k in ks:
        hcopy(k).start()
    for k in ks:
        hwait(k).wait_recv()
    for k in ks:
        hcopy(k).wait_send()

    hidden = hall[:, 0:PAD, :].reshape(flat, hid)
    grads = hall[:, PAD:, :].reshape(flat, hid)

    def halves(c):
        m = jnp.dot(
            hidden,
            w_out_ref[:, pl.ds(pl.multiple_of(c * half_out, 128), half_out)],
            preferred_element_type=F32,
        )
        g = lax.dot_general(
            grads,
            w_in_ref[pl.ds(pl.multiple_of(c * half_in, 16), half_in), :],
            (((1,), (1,)), ((), ())),
            preferred_element_type=F32,
        )
        return m.reshape(n_dp, PAD, half_out), g.reshape(n_dp, PAD, half_in)

    wide = csend.shape[2]
    spare = jnp.zeros((n_dp, PAD, wide - half_out - half_in), F32)
    m, g = halves(p.co)
    csend[:, :, 0:half_out] = m.astype(BF16)
    csend[:, :, half_out:] = jnp.concatenate([g, spare], axis=2).astype(BF16)
    to_core = rcopy(csend, crecv, sc, rc, p.C)
    to_core.start()
    m, g = halves(p.c)
    pieces[:, :, 0:half_out] = m
    pieces[:, :, half_out:] = jnp.concatenate([g, spare], axis=2)
    to_core.wait_recv()
    parts = ((slice(None), slice(0, half_out)), (slice(None), slice(half_out, wide)))

    def piece(y, x, part):
        j = y * 2 + x
        rows_, cols_ = parts[part]
        return pieces[j, rows_, cols_] + crecv[j, rows_, cols_].astype(F32)

    rs = Scatter(p, sb, rb, parts, srs, rrs, piece)
    rs.first(0)
    rs.first(1)
    rs.second(0)
    rs.second(1)
    rs.third()
    for part in range(2):
        fin[parts[part]] = rs.last(part)

    over = rcopy(fin, finr, sperm, rperm, swap)

    @pl.when(stays)
    def _():
        finr[...] = fin[...]

    @pl.when(jnp.logical_not(stays))
    def _():
        over.start()

    to_core.wait_send()
    rs.drain()

    @pl.when(jnp.logical_not(stays))
    def _():
        over.wait_recv()
        over.wait_send()

    gg[p.me] = finr[:, half_out : half_out + half_in]
    ag = Gather(p, gg, PAD, sag, rag)
    ag.start()

    merged = (finr[0:rows, 0:half_out] + b_out_ref[...]).astype(BF16)
    tokens = text_ref.shape[0]
    token = lax.broadcasted_iota(jnp.int32, (tokens, rows), 0)
    slot = lax.broadcasted_iota(jnp.int32, (tokens, rows), 1)
    select = jnp.where(
        jnp.logical_and(place_ref[...] == token, slot < count_ref[0]), 1.0, 0.0
    ).astype(F32)
    image = jnp.sum(select, axis=1, keepdims=True)
    picked = jnp.dot(select.astype(BF16), merged, preferred_element_type=F32)
    start_ref[...] = jnp.where(image > 0.5, picked, text_ref[...].astype(F32)).astype(BF16)

    ag.first()
    ag.second()
    ag.third()
    for j in range(8):
        ag.wait_all(p.sid(j // 2, lax.rem(j, 2), p.co))
    ag.drain()
    per = vit // half_in
    for g in range(groups):
        cols = slice(g * vit, (g + 1) * vit)
        unit, rstd = norm_parts(patches_ref[:, cols].astype(F32))
        down = jnp.concatenate([gg[g * per + i] for i in range(per)], axis=1)[0:rows] * gain
        mean = jnp.mean(down, axis=-1, keepdims=True)
        along = jnp.mean(down * unit, axis=-1, keepdims=True)
        pg_ref[:, cols] = rstd * (down - mean - unit * along)


def merger(count, patches, grads, gain, shift, w_in, b_in, w_out, b_out, place, text):
    n_dp = 8
    xw, gw, hid = w_in.shape[0], w_out.shape[1], w_in.shape[1]
    wide = gw // 2 + ((xw // 2 + 127) // 128) * 128
    dma = pltpu.SemaphoreType.DMA
    vm = pl.BlockSpec(memory_space=pltpu.VMEM)
    return pl.pallas_call(
        merger_kernel,
        out_shape=(
            jax.ShapeDtypeStruct(text.shape, BF16),
            jax.ShapeDtypeStruct(patches.shape, F32),
        ),
        in_specs=[pl.BlockSpec(memory_space=pltpu.SMEM)] + [vm] * 10,
        out_specs=(vm, vm),
        scratch_shapes=[
            pltpu.VMEM((PAD, patches.shape[1]), BF16),
            pltpu.VMEM((PAD, grads.shape[1]), BF16),
            pltpu.VMEM((n_dp, PAD, xw), BF16),
            pltpu.VMEM((n_dp, PAD, gw), BF16),
            pltpu.VMEM((n_dp, 2 * PAD, hid), BF16),
            pltpu.VMEM((n_dp, 2 * PAD, hid), BF16),
            pltpu.VMEM((n_dp, 2 * PAD, hid), BF16),
            pltpu.VMEM((n_dp, PAD, wide), BF16),
            pltpu.VMEM((n_dp, PAD, wide), BF16),
            pltpu.VMEM((n_dp, PAD, wide), F32),
            pltpu.VMEM((7, PAD, wide), BF16),
            pltpu.VMEM((7, PAD, wide), BF16),
            pltpu.VMEM((PAD, wide), F32),
            pltpu.VMEM((PAD, wide), F32),
            pltpu.VMEM((16, PAD, xw // 2), F32),
            dma((n_dp,)),
            dma((n_dp,)),
            dma((n_dp,)),
            dma((n_dp,)),
            dma((n_dp,)),
            dma((n_dp,)),
            dma((n_dp,)),
            dma((n_dp,)),
            dma,
            dma,
            dma((14,)),
            dma((14,)),
            dma,
            dma,
            dma((GATHER_SENDS,)),
            dma((32,)),
        ],
        compiler_params=pltpu.CompilerParams(
            collective_id=0, has_side_effects=True, vmem_limit_bytes=48 * 2**20
        ),
    )(count, patches, grads, gain, shift, w_in, b_in, w_out, b_out, place, text)


def layers_kernel(
    start_ref,
    gain_ref,
    inv_ref,
    mask_ref,
    cos_ref,
    sin_ref,
    cos_t_ref,
    sin_t_ref,
    q_hbm,
    kv_hbm,
    o_hbm,
    out_ref,
    gath,
    qv,
    kvv,
    wv,
    acc_q,
    acc_kv,
    acc_ss,
    qb,
    kvx,
    attb,
    sb,
    rb,
    lq,
    lkv,
    lo,
    so,
    ro,
    sag,
    rag,
    skv,
    rkv,
    sat,
    rat,
    srs,
    rrs,
):
    p = Place()
    layers = q_hbm.shape[0]
    tokens = start_ref.shape[0]
    share = start_ref.shape[1]
    half = tokens // 2
    barrier_with((p.U, p.Dn, p.X, p.C, p.XC))

    def block(l, s):
        return pl.ds(pl.multiple_of(s * share, 128), share)

    def loads(l):
        out = [
            pltpu.make_async_copy(q_hbm.at[l], qv.at[l], lq.at[l]),
            pltpu.make_async_copy(kv_hbm.at[l, 0], kvv.at[l, 0], lkv.at[l, 0]),
            pltpu.make_async_copy(kv_hbm.at[l, 1], kvv.at[l, 1], lkv.at[l, 1]),
        ]
        return out

    rows_of = pl.ds(pl.multiple_of(p.c * 256, 16), 256)

    def own_o(l, j):
        s = p.sid(j // 2, lax.rem(j, 2), p.c)
        return pltpu.make_async_copy(
            o_hbm.at[l, :, block(l, s)], wv.at[l, j, rows_of, :], lo.at[l, j]
        )

    def give_o(l, j):
        s = p.sid(j // 2, lax.rem(j, 2), p.co)
        return rcopy(
            o_hbm.at[l, :, block(l, s)],
            wv.at[l, j, rows_of, :],
            so.at[l, j],
            ro.at[l, j],
            p.C,
        )

    for cp in loads(0):
        cp.start()
    out_ref[...] = start_ref[...].astype(F32)

    def layer(l, carry):
        gain = gain_ref[l, :, block(l, p.me)]
        gath[p.me] = (out_ref[...] * gain).astype(BF16)
        ag = Gather(p, gath, tokens, sag, rag)
        ag.start()

        @pl.when(l == 0)
        def _():
            for j in range(8):
                own_o(0, j).start()
                give_o(0, j).start()
            for k in range(1, layers):
                for cp in loads(k):
                    cp.start()
                for j in range(8):
                    own_o(k, j).start()
                    give_o(k, j).start()

        acc_q[...] = jnp.zeros_like(acc_q)
        acc_kv[...] = jnp.zeros_like(acc_kv)
        acc_ss[...] = jnp.zeros_like(acc_ss)
        for cp in loads(l):
            cp.wait()

        def project(s):
            g = gath[s]
            acc_q[...] += jnp.dot(g, qv[l, block(l, s), :], preferred_element_type=F32)
            for i in range(2):
                acc_kv[pl.ds(i * 32, 32), :] += lax.dot_general(
                    kvv[l, i, :, block(l, s)],
                    g,
                    (((1,), (1,)), ((), ())),
                    preferred_element_type=F32,
                )
            gf = g.astype(F32)
            sq = gf * gf * inv_ref[l, :, block(l, s)]
            fold = sq[:, 0:128]
            for at in range(128, share, 128):
                fold = fold + sq[:, at : at + 128]
            acc_ss[...] += fold

        project(p.me)
        ag.first()
        s = p.sid(p.y, p.x, p.co)
        ag.wait_all(s)
        project(s)
        project(p.sid(p.y, p.xo, p.c))
        ag.second()
        project(p.sid(p.yd, p.x, p.c))
        project(p.sid(p.yu, p.x, p.c))
        ag.third()
        for y, x in ((p.y, p.xo), (p.yd, p.x), (p.yu, p.x)):
            s = p.sid(y, x, p.co)
            ag.wait_all(s)
            project(s)
        for y, x in ((p.ya, p.x), (p.yd, p.xo), (p.yu, p.xo), (p.ya, p.xo)):
            project(p.sid(y, x, p.c))
        for y, x in ((p.ya, p.x), (p.yd, p.xo), (p.yu, p.xo), (p.ya, p.xo)):
            s = p.sid(y, x, p.co)
            ag.wait_all(s)
            project(s)

        total = jnp.sum(acc_ss[...], axis=1, keepdims=True)
        factor = lax.rsqrt(jnp.broadcast_to(total, (tokens, 128)) * (1.0 / D) + rms_eps)
        factor_t = jnp.transpose(factor)
        kvx[p.mp] = (acc_kv[...] * factor_t[0:64, :]).astype(BF16)

        def kv_copy(i, dev):
            return rcopy(kvx.at[p.mp], kvx.at[p.mp], skv.at[i], rkv.at[p.mp], dev)

        kv_to = [kv_copy(0, p.X), kv_copy(1, p.XC), kv_copy(2, p.C)]
        for cp in kv_to:
            cp.start()
        for hh in range(2):
            cols = slice(hh * 128, (hh + 1) * 128)
            q = acc_q[:, cols] * factor
            qb[:, cols] = (q * cos_ref[...] + pltpu.roll(q, 64, 1) * sin_ref[...]).astype(BF16)
        ag.drain()
        for m in (p.xo * 2 + p.c, p.xo * 2 + p.co, p.x * 2 + p.co):
            rcopy(kvx.at[m], kvx.at[m], skv.at[0], rkv.at[m], p.C).wait_recv()
        low = jnp.concatenate([kvx[0, 0:32, :], kvx[1, 0:32, :]], axis=0).astype(F32)
        high = jnp.concatenate([kvx[2, 0:32, :], kvx[3, 0:32, :]], axis=0).astype(F32)
        cos_t, sin_t = cos_t_ref[...], sin_t_ref[...]
        keys = jnp.concatenate(
            [low * cos_t - high * sin_t, high * cos_t + low * sin_t], axis=0
        ).astype(BF16)
        values = jnp.concatenate([kvx[m, 32:64, :] for m in range(4)], axis=0)

        def attend(part):
            rows = slice(part * half, (part + 1) * half)
            seen = (part + 1) * half
            for hh in range(2):
                cols = slice(hh * 128, (hh + 1) * 128)
                scores = jnp.dot(qb[rows, cols], keys[:, 0:seen], preferred_element_type=F32) * (
                    1.0 / math.sqrt(HEAD_DIM)
                )
                scores = jnp.where(mask_ref[rows, 0:seen] > 0.5, scores, -1e30)
                top = jnp.max(scores, axis=-1, keepdims=True)
                weights = jnp.exp(scores - top)
                weights = (weights / jnp.sum(weights, axis=-1, keepdims=True)).astype(BF16)
                attb[p.c, rows, cols] = lax.dot_general(
                    weights,
                    values[:, 0:seen],
                    (((1,), (1,)), ((), ())),
                    preferred_element_type=F32,
                ).astype(BF16)

        def at_copy(part, c):
            view = attb.at[c, pl.ds(part * half, half), :]
            return rcopy(view, view, sat.at[part], rat.at[part], p.C)

        for j in range(8):
            own_o(l, j).wait()
            give_o(l, j).wait_recv()

        def piece(y, x, part):
            j = y * 2 + x
            rows = pl.ds(part * half, half)
            return jnp.dot(
                attb[0, rows, :], wv[l, j, 0:256, :], preferred_element_type=F32
            ) + jnp.dot(attb[1, rows, :], wv[l, j, 256:512, :], preferred_element_type=F32)

        parts = tuple((slice(i * half, (i + 1) * half), slice(None)) for i in range(2))
        rs = Scatter(p, sb, rb, parts, srs, rrs, piece)
        for part in range(2):
            attend(part)
            at_copy(part, p.c).start()
        for part in range(2):
            at_copy(part, p.co).wait_recv()
            rs.first(part)
        rs.second(0)
        rs.second(1)
        rs.third()
        for part in range(2):
            rows = parts[part][0]
            out_ref[rows, :] += rs.last(part)
        rs.drain()
        for cp in kv_to:
            cp.wait_send()
        for part in range(2):
            at_copy(part, p.c).wait_send()
        for j in range(8):
            give_o(l, j).wait_send()
        return carry

    lax.fori_loop(0, layers, layer, 0)


def layers_call(start, gain, inv, mask, cos, sin, cos_t, sin_t, q_weight, kv_weight, o_weight):
    tokens, share = start.shape
    layers = q_weight.shape[0]
    dma = pltpu.SemaphoreType.DMA
    vm = pl.BlockSpec(memory_space=pltpu.VMEM)
    hbm = pl.BlockSpec(memory_space=pl.ANY)
    return pl.pallas_call(
        layers_kernel,
        out_shape=jax.ShapeDtypeStruct((tokens, share), F32),
        in_specs=[vm] * 8 + [hbm] * 3,
        out_specs=vm,
        scratch_shapes=[
            pltpu.VMEM((16, tokens, share), BF16),
            pltpu.VMEM(q_weight.shape, BF16),
            pltpu.VMEM(kv_weight.shape, BF16),
            pltpu.VMEM((layers, 8, 512, share), BF16),
            pltpu.VMEM((tokens, 256), F32),
            pltpu.VMEM((64, tokens), F32),
            pltpu.VMEM((tokens, 128), F32),
            pltpu.VMEM((tokens, 256), BF16),
            pltpu.VMEM((4, 64, tokens), BF16),
            pltpu.VMEM((2, tokens, 256), BF16),
            pltpu.VMEM((7, tokens, share), BF16),
            pltpu.VMEM((7, tokens, share), BF16),
            dma((layers,)),
            dma((layers, 2)),
            dma((layers, 8)),
            dma((layers, 8)),
            dma((layers, 8)),
            dma((GATHER_SENDS,)),
            dma((32,)),
            dma((3,)),
            dma((4,)),
            dma((2,)),
            dma((2,)),
            dma((14,)),
            dma((14,)),
        ],
        compiler_params=pltpu.CompilerParams(
            collective_id=1, has_side_effects=True, vmem_limit_bytes=60 * 2**20
        ),
    )(start, gain, inv, mask, cos, sin, cos_t, sin_t, q_weight, kv_weight, o_weight)


def local(
    patches,
    ln_gain,
    ln_shift,
    w_in,
    b_in,
    w_out,
    b_out,
    place,
    image_counts,
    text_rows,
    segments,
    norm_gain,
    q_weight,
    kv_weight,
    o_weight,
    grad_rows,
):
    start, patch_grads = merger(
        image_counts,
        patches,
        grad_rows,
        ln_gain.astype(F32)[None],
        ln_shift.astype(F32)[None],
        w_in,
        b_in.astype(F32)[None],
        w_out,
        b_out.astype(F32)[None],
        place[None],
        text_rows,
    )
    tokens = text_rows.shape[0]
    index = jnp.arange(tokens, dtype=jnp.int32)
    ids = segments[0]
    allowed = (ids[:, None] == ids[None, :]) & (index[None, :] <= index[:, None])
    mask = allowed.astype(F32)
    positions = jnp.sum(mask, axis=1) - 1.0
    half = HEAD_DIM // 2
    inv_freq = rope_base ** (-2.0 * jnp.arange(half, dtype=F32) / HEAD_DIM)
    angles = positions[:, None] * inv_freq[None, :]
    cos, sin = jnp.cos(angles), jnp.sin(angles)
    gain = norm_gain.astype(F32)[:, None, :]
    out = layers_call(
        start,
        gain,
        1.0 / (gain * gain),
        mask,
        jnp.concatenate([cos, cos], axis=1),
        jnp.concatenate([-sin, sin], axis=1),
        cos.T,
        sin.T,
        q_weight,
        kv_weight,
        o_weight,
    )
    return (out, patch_grads)


def solution(mesh):
    in_specs = (
        P("dp", None),
        P(),
        P(),
        P("dp", ("sec", "mp")),
        P(("sec", "mp")),
        P(("sec", "mp"), "dp"),
        P(("sec", "mp")),
        P("dp"),
        P("dp"),
        P("dp", ("sec", "mp")),
        P("dp", None),
        P(),
        P(None, None, ("sec", "mp")),
        P(None, None, ("sec", "mp"), None),
        P(None, ("sec", "mp"), None),
        P("dp", None),
    )
    out_specs = (P("dp", ("sec", "mp")), P("dp", None))
    return jax.shard_map(local, mesh=mesh, in_specs=in_specs, out_specs=out_specs, check_vma=False)
```

```python
import functools
import math

import jax
import jax.numpy as jnp
from jax import lax
from jax.experimental import pallas as pl
from jax.experimental.pallas import tpu as pltpu
from jax.sharding import PartitionSpec as P

D = 8192
HEAD_DIM = 128
PAD = 48

ln_eps = 1e-06
rms_eps = 1e-06
rope_base = 1000000.0

MESH = pl.DeviceIdType.MESH
F32 = jnp.float32
BF16 = jnp.bfloat16


class Place:
    def __init__(self):
        self.y = lax.axis_index("sec")
        self.d = lax.axis_index("dp")
        mp = lax.axis_index("mp")
        self.mp = mp
        self.x = mp // 2
        self.c = lax.rem(mp, 2)
        self.yu = lax.rem(self.y + 1, 4)
        self.yd = lax.rem(self.y + 3, 4)
        self.ya = lax.rem(self.y + 2, 4)
        self.xo = 1 - self.x
        self.co = 1 - self.c
        self.U = self.dev(self.yu, self.x, self.c)
        self.Dn = self.dev(self.yd, self.x, self.c)
        self.X = self.dev(self.y, self.xo, self.c)
        self.C = self.dev(self.y, self.x, self.co)
        self.XC = self.dev(self.y, self.xo, self.co)
        self.me = self.sid(self.y, self.x, self.c)

    def dev(self, y, x, c):
        return {"sec": y, "dp": self.d, "mp": x * 2 + c}

    def sid(self, y, x, c):
        return y * 4 + x * 2 + c


def rcopy(src, dst, ssem, rsem, dev):
    return pltpu.make_async_remote_copy(
        src_ref=src, dst_ref=dst, send_sem=ssem, recv_sem=rsem, device_id=dev, device_id_type=MESH
    )


class Gather:
    def __init__(self, place, buf, chunks, ssem, rsem):
        self.p, self.buf, self.chunks = place, buf, chunks
        self.ssem, self.rsem = ssem, rsem
        self.sent = []

    def view(self, s, h):
        return self.buf.at[s].at[self.chunks[h]]

    def send(self, s, h, *devs):
        for dev in devs:
            k = len(self.sent)
            cp = rcopy(
                self.view(s, h), self.view(s, h), self.ssem.at[k], self.rsem.at[s * 2 + h], dev
            )
            cp.start()
            self.sent.append(cp)

    def wait(self, s, h):
        rcopy(
            self.view(s, h), self.view(s, h), self.ssem.at[0], self.rsem.at[s * 2 + h], self.p.C
        ).wait_recv()

    def wait_all(self, s):
        self.wait(s, 0)
        self.wait(s, 1)

    def steps(self, use):
        p = self.p
        own = p.c
        other = p.co

        def late(y, x):
            s = p.sid(y, x, other)
            self.wait_all(s)
            use(s)

        self.send(p.me, 0, p.X, p.U)
        self.send(p.me, 1, p.X, p.Dn)
        self.send(p.me, 1, p.U)
        self.send(p.me, 0, p.Dn, p.C)
        self.send(p.me, 1, p.C)
        use(p.me)
        yield 2.5
        up, down = p.sid(p.yu, p.x, own), p.sid(p.yd, p.x, own)
        self.wait(down, 0)
        self.send(down, 0, p.U, p.C)
        self.wait(up, 1)
        self.send(up, 1, p.Dn, p.C)
        yield 0.5
        beside = p.sid(p.y, p.xo, own)
        for h in range(2):
            self.wait(beside, h)
            self.send(beside, h, p.U, p.Dn, p.C)
        use(beside)
        yield 1.0
        self.wait(down, 1)
        self.send(down, 1, p.C)
        self.wait(up, 0)
        self.send(up, 0, p.C)
        use(down)
        use(up)
        late(p.y, p.x)
        yield 1.5
        far = p.sid(p.ya, p.x, own)
        for h in range(2):
            self.wait(far, h)
            self.send(far, h, p.X, p.C)
        use(far)
        late(p.y, p.xo)
        yield 1.0
        for y in (p.yd, p.yu):
            s = p.sid(y, p.xo, own)
            for h in range(2):
                self.wait(s, h)
                self.send(s, h, p.C)
            use(s)
        late(p.yd, p.x)
        late(p.yu, p.x)
        yield 1.0
        late(p.ya, p.x)
        s = p.sid(p.ya, p.xo, own)
        for h in range(2):
            self.wait(s, h)
            self.send(s, h, p.C)
        use(s)
        late(p.yd, p.xo)
        late(p.yu, p.xo)
        yield 1.0
        late(p.ya, p.xo)
        for cp in self.sent:
            cp.wait_send()


GATHER_SENDS = 30


class Scatter:
    def __init__(self, place, sb, rb, parts, ssem, rsem, piece):
        self.p, self.sb, self.rb, self.parts = place, sb, rb, parts
        self.ssem, self.rsem, self.piece = ssem, rsem, piece
        self.sent = []

    def copy(self, i, part, dev):
        return rcopy(
            self.sb.at[i].at[self.parts[part]],
            self.rb.at[i].at[self.parts[part]],
            self.ssem.at[i * 2 + part],
            self.rsem.at[i * 2 + part],
            dev,
        )

    def send(self, i, part, dev, value):
        self.sb.at[i][self.parts[part]] = value.astype(BF16)
        cp = self.copy(i, part, dev)
        cp.start()
        self.sent.append(cp)

    def both(self, i, dev, y, x):
        for part, value in enumerate(self.piece(y, x, None)):
            self.send(i, part, dev, value)

    def got(self, i, part):
        self.copy(i, part, self.p.C).wait_recv()
        return self.rb.at[i][self.parts[part]].astype(F32)

    def steps(self, finish, lag=1.0):
        p, piece = self.p, self.piece
        self.both(0, p.X, p.ya, p.xo)
        self.both(1, p.U, p.yu, p.xo)
        self.both(2, p.Dn, p.yd, p.xo)
        self.send(5, 1, p.U, piece(p.yu, p.x, 1))
        self.send(6, 0, p.Dn, piece(p.yd, p.x, 0))
        yield 2.0 * lag
        own = piece(p.ya, p.x, None)
        for part in range(2):
            self.send(3, part, (p.U, p.Dn)[part], own[part] + self.got(0, part))
        yield 1.0 * lag
        own = piece(p.y, p.xo, None)
        for part in range(2):
            self.send(4, part, p.X, own[part] + self.got(1, part) + self.got(2, part))
        yield 1.5 * lag
        own = piece(p.yu, p.x, 0)
        self.send(5, 0, p.U, own + self.got(3, 0))
        own = piece(p.yd, p.x, 1)
        self.send(6, 1, p.Dn, own + self.got(3, 1))
        yield 2.5 * lag
        own = piece(p.y, p.x, None)
        for part in range(2):
            finish(part, own[part] + self.got(4, part) + self.got(5, part) + self.got(6, part))
        for cp in self.sent:
            cp.wait_send()


def interleave(*streams):
    clock = [[start, i, stream] for i, (start, stream) in enumerate(streams)]
    while clock:
        now = min(clock, key=lambda item: (item[0], item[1]))
        try:
            now[0] += next(now[2])
        except StopIteration:
            clock.remove(now)


def norm_parts(group):
    center = group - jnp.mean(group, axis=-1, keepdims=True)
    spread = jnp.mean(center * center, axis=-1, keepdims=True)
    rstd = lax.rsqrt(spread + ln_eps)
    return center * rstd, rstd


VIT_AT, SHIFT_AT, B_OUT_AT, PLACE_AT, B_IN_AT = 0, 1280, 2560, 3072, 3200


def step_kernel(
    count_ref,
    small_ref,
    seg_ref,
    gain_ref,
    patches_hbm,
    grads_hbm,
    w_in_hbm,
    w_out_hbm,
    text_hbm,
    q_hbm,
    kv_hbm,
    o_hbm,
    out_ref,
    pg_ref,
    patches_ref,
    grads_ref,
    w_in_ref,
    w_out_ref,
    text_ref,
    lin,
    xs,
    gs,
    xall,
    gall,
    psend,
    precv,
    hall,
    pre_ref,
    fsend,
    frecv,
    fpiece,
    fsb,
    frb,
    bsend,
    brecv,
    bpiece,
    bsb,
    brb,
    ffin,
    ffinr,
    bfin,
    bfinr,
    gg,
    gimg,
    gath,
    qv,
    kvv,
    wv,
    gains,
    invs,
    mask_ref,
    cos_ref,
    sin_ref,
    cos_t_ref,
    sin_t_ref,
    acc_q,
    acc_kv,
    acc_ss,
    img_q,
    img_kv,
    img_ss,
    qb,
    kvx,
    attb,
    sb,
    rb,
    sx,
    rx,
    sf,
    sp,
    rp,
    sh,
    rh,
    sc,
    rc,
    srs,
    rrs,
    sperm,
    rperm,
    sag,
    rag,
    simg,
    rimg,
    lq,
    lkv,
    lo,
    so,
    ro,
    stx,
    rtx,
    skv,
    rkv,
    sat,
    rat,
    sls,
    rls,
):
    p = Place()
    n_dp = xall.shape[0]
    rows = patches_ref.shape[0]
    vit = 1280
    groups = patches_ref.shape[1] // vit
    xw, gw, hid = xall.shape[2], gall.shape[2], w_in_ref.shape[1]
    half_out, half_in = gw // 2, xw // 2
    layers = q_hbm.shape[0]
    tokens, share = text_ref.shape
    half = tokens // 2
    flat = n_dp * PAD
    ks = list(range(1, n_dp))

    def peer(k):
        d = lax.rem(p.d + k, n_dp)
        return d, {"sec": p.y, "dp": d, "mp": p.mp}

    swap_dp = p.me // 2
    swap_s = 2 * p.d + lax.rem(p.me, 2)
    swap = {"sec": swap_s // 4, "dp": swap_dp, "mp": lax.rem(swap_s, 4)}
    stays = jnp.logical_and(swap_dp == p.d, swap_s == p.me)
    moves = jnp.logical_not(stays)

    sem = pltpu.get_barrier_semaphore()
    for dev in [peer(k)[1] for k in ks] + [p.U, p.Dn, p.X, p.C, p.XC, swap]:
        pl.semaphore_signal(sem, inc=1, device_id=dev, device_id_type=MESH)

    def block(s):
        return pl.ds(pl.multiple_of(s * share, 128), share)

    def load(i):
        src, dst = (
            (patches_hbm, patches_ref),
            (text_hbm, text_ref),
            (w_in_hbm, w_in_ref),
            (w_out_hbm, w_out_ref),
            (grads_hbm, grads_ref),
        )[i]
        return pltpu.make_async_copy(src, dst, lin.at[i])

    def loads(l):
        return [
            pltpu.make_async_copy(q_hbm.at[l], qv.at[l], lq.at[l]),
            pltpu.make_async_copy(kv_hbm.at[l, 0], kvv.at[l, 0], lkv.at[l, 0]),
            pltpu.make_async_copy(kv_hbm.at[l, 1], kvv.at[l, 1], lkv.at[l, 1]),
        ]

    rows_of = pl.ds(pl.multiple_of(p.c * 256, 16), 256)

    def own_o(l, j):
        s = p.sid(j // 2, j % 2, p.c)
        return pltpu.make_async_copy(
            o_hbm.at[l, :, block(s)], wv.at[l, j, rows_of, :], lo.at[l, j]
        )

    def give_o(l, j):
        s = p.sid(j // 2, j % 2, p.co)
        return rcopy(
            o_hbm.at[l, :, block(s)], wv.at[l, j, rows_of, :], so.at[l, j], ro.at[l, j], p.C
        )

    for i in range(5):
        load(i).start()
    for cp in loads(0):
        cp.start()

    for l in range(layers):
        g = gain_ref[l : l + 1, :].astype(F32)
        gains[l] = g
        invs[l] = 1.0 / (g * g)
    ln_gain = small_ref[:, VIT_AT:SHIFT_AT]
    load(0).wait()
    for g in range(groups):
        cols = slice(g * vit, (g + 1) * vit)
        unit, _ = norm_parts(patches_ref[:, cols].astype(F32))
        scaled = unit * ln_gain + small_ref[:, SHIFT_AT:B_OUT_AT]
        xs[:, cols] = jnp.concatenate([scaled, jnp.zeros((PAD - rows, vit), F32)], 0).astype(BF16)
    load(1).wait()
    gain0 = gains[0, :, block(p.me)]
    for h in range(2):
        rows_h = slice(h * half, (h + 1) * half)
        gath[h, p.me] = (text_ref[rows_h, :].astype(F32) * gain0).astype(BF16)
    pl.semaphore_wait(sem, n_dp - 1 + 6)


    def spread(way, src, dst, width):
        def put(k):
            d, dev = peer(k)
            view = src.at[:, pl.ds(pl.multiple_of(d * width, 128), width)]
            return rcopy(view, dst.at[p.d], sx.at[way, k], rx.at[way, p.d], dev)

        def pass_on(k):
            d, _ = peer(k)
            return rcopy(dst.at[d], dst.at[d], sf.at[way, k], rx.at[way, d], p.C)

        def on_core(c, body):
            @pl.when(p.c == c)
            def _():
                body([k for k in ks if k % 2 == c])

        for c in range(2):
            on_core(c, lambda mine: [put(k).start() for k in mine])
        dst[p.d] = src[:, pl.ds(pl.multiple_of(p.d * width, 128), width)]
        yield 5.0
        for c in range(2):

            def arrive(mine):
                for k in mine:
                    pass_on(k).wait_recv()
                    pass_on(k).start()

            on_core(c, arrive)
        yield 1.5
        for c in range(2):

            def finish(mine):
                for k in ks:
                    if k not in mine:
                        pass_on(k).wait_recv()
                for k in mine:
                    put(k).wait_send()
                    pass_on(k).wait_send()

            on_core(c, finish)

    def back(way, term, done):
        psend[way] = term().astype(BF16).reshape(n_dp, PAD, hid)

        def put(k):
            d, dev = peer(k)
            return rcopy(
                psend.at[way, d], precv.at[way, p.d], sp.at[way, k], rp.at[way, p.d], dev
            )

        def take(k):
            d, dev = peer(k)
            return rcopy(psend.at[way, d], precv.at[way, d], sp.at[way, k], rp.at[way, d], dev)

        for k in ks:
            put(k).start()
        yield 6.0
        total = psend[way, p.d].astype(F32)
        for k in ks:
            take(k).wait_recv()
            total = total + precv[way, peer(k)[0]].astype(F32)
        done(total)
        for k in ks:
            put(k).wait_send()

    def share_units(way, value):
        hall[way, p.d] = value.astype(BF16)

        def put(k):
            return rcopy(
                hall.at[way, p.d], hall.at[way, p.d], sh.at[way, k], rh.at[way, p.d], peer(k)[1]
            )

        def take(k):
            d, dev = peer(k)
            return rcopy(hall.at[way, d], hall.at[way, d], sh.at[way, k], rh.at[way, d], dev)

        for k in ks:
            put(k).start()
        yield 5.0
        for k in ks:
            take(k).wait_recv()
        for k in ks:
            put(k).wait_send()

    def gather_sums(way, term, csend, crecv, pieces, s_buf, r_buf, fin, finr):
        csend[...] = term(p.co).astype(BF16)
        over = rcopy(csend, crecv, sc.at[way], rc.at[way], p.C)
        over.start()
        pieces[...] = term(p.c)
        yield 1.0
        over.wait_recv()
        wide = csend.shape[2]
        parts = ((slice(None), slice(0, 256)), (slice(None), slice(256, wide)))

        def piece(y, x, part):
            j = y * 2 + x
            out = []
            for r, c in parts:
                out.append(pieces[j, r, c] + crecv[j, r, c].astype(F32))
            return out if part is None else out[part]

        def finish(part, total):
            fin[parts[part]] = total.astype(fin.dtype)

        rs = Scatter(p, s_buf, r_buf, parts, srs.at[way], rrs.at[way], piece)
        yield from rs.steps(finish, 0.9)
        over.wait_send()
        cross = rcopy(fin, finr, sperm.at[way], rperm.at[way], swap)

        @pl.when(stays)
        def _():
            finr[...] = fin[...]

        @pl.when(moves)
        def _():
            cross.start()

        yield 4.0

        @pl.when(moves)
        def _():
            cross.wait_recv()
            cross.wait_send()

    def units(way):
        return hall[way].reshape(flat, hid)

    def forward():
        yield from spread(0, xs, xall, xw)
        load(2).wait()
        load(3).wait()

        def first():
            return jnp.dot(xall[...].reshape(flat, xw), w_in_ref[...], preferred_element_type=F32)

        def keep(total):
            pre_ref[...] = total + small_ref[:, B_IN_AT : B_IN_AT + hid]

        yield from back(0, first, keep)
        pre = pre_ref[...]
        yield from share_units(
            0, pre * 0.5 * (1.0 + lax.erf(pre * (1.0 / math.sqrt(2.0))))
        )

        def second(c):
            at = pl.ds(pl.multiple_of(c * half_out, 128), half_out)
            out = jnp.dot(units(0), w_out_ref[:, at], preferred_element_type=F32)
            return out.reshape(n_dp, PAD, half_out)

        yield from gather_sums(0, second, fsend, frecv, fpiece, fsb, frb, ffin, ffinr)
        merged = ffinr[...].astype(F32) + small_ref[:, B_OUT_AT:PLACE_AT]
        merged = merged.astype(BF16)
        gimg[p.me] = (merged.astype(F32) * gain0).astype(BF16)
        img_q[...] = jnp.zeros_like(img_q)
        img_kv[...] = jnp.zeros_like(img_kv)
        img_ss[...] = jnp.zeros_like(img_ss)
        chunks = tuple((slice(None), slice(i * 256, (i + 1) * 256)) for i in range(2))
        ag = Gather(p, gimg, chunks, simg, rimg)
        steps = ag.steps(lambda s: project(0, s, gimg[s], img_q, img_kv, img_ss))
        yield next(steps)
        for h in range(2):
            rows_h = slice(h * half, (h + 1) * half)
            chosen = select(h)
            picked = jnp.dot(chosen.astype(BF16), merged[0:rows], preferred_element_type=F32)
            image = jnp.sum(chosen, axis=1, keepdims=True) > 0.5
            out_ref[rows_h, :] = jnp.where(image, picked, text_ref[rows_h, :].astype(F32))
        yield from steps

    def backward():
        load(4).wait()
        live = lax.broadcasted_iota(jnp.int32, (rows, 1), 0) < count_ref[0]
        for at in range(0, gs.shape[1], 1024):
            g = jnp.where(live, grads_ref[:, at : at + 1024].astype(F32), 0.0)
            gs[:, at : at + 1024] = jnp.concatenate(
                [g, jnp.zeros((PAD - rows, 1024), F32)], 0
            ).astype(BF16)
        yield from spread(1, gs, gall, gw)
        box = []

        def first():
            return lax.dot_general(
                gall[...].reshape(flat, gw),
                w_out_ref[...],
                (((1,), (1,)), ((), ())),
                preferred_element_type=F32,
            )

        def keep(total):
            pre = pre_ref[...]
            cdf = 0.5 * (1.0 + lax.erf(pre * (1.0 / math.sqrt(2.0))))
            pdf = jnp.exp(-0.5 * pre * pre) * (1.0 / math.sqrt(2.0 * math.pi))
            box.append(total * (cdf + pre * pdf))

        yield from back(1, first, keep)
        yield from share_units(1, box[0])
        wide = bpiece.shape[2]

        def second(c):
            at = pl.ds(pl.multiple_of(c * half_in, 16), half_in)
            out = lax.dot_general(
                units(1), w_in_ref[at, :], (((1,), (1,)), ((), ())), preferred_element_type=F32
            ).reshape(n_dp, PAD, half_in)
            return jnp.concatenate([out, jnp.zeros((n_dp, PAD, wide - half_in), F32)], axis=2)

        yield from gather_sums(1, second, bsend, brecv, bpiece, bsb, brb, bfin, bfinr)
        gg[p.me] = bfinr[...]
        chunks = ((slice(None), slice(0, 256)), (slice(None), slice(256, wide)))
        yield from Gather(p, gg, chunks, sag, rag).steps(lambda s: None)
        per = vit // half_in
        for g in range(groups):
            cols = slice(g * vit, (g + 1) * vit)
            unit, rstd = norm_parts(patches_ref[:, cols].astype(F32))
            down = [gg[g * per + i, 0:rows, 0:half_in].astype(F32) for i in range(per)]
            down = jnp.concatenate(down, axis=1) * ln_gain
            mean = jnp.mean(down, axis=-1, keepdims=True)
            along = jnp.mean(down * unit, axis=-1, keepdims=True)
            pg_ref[:, cols] = rstd * (down - mean - unit * along)


    def project(l, s, g, q, kv, ss):
        q[...] += jnp.dot(g, qv[l, block(s), :], preferred_element_type=F32)
        for i in range(2):
            kv[pl.ds(i * 32, 32), :] += lax.dot_general(
                kvv[l, i, :, block(s)], g, (((1,), (1,)), ((), ())), preferred_element_type=F32
            )
        gf = g.astype(F32)
        sq = gf * gf * invs[l, :, block(s)]
        fold = sq[:, 0:128]
        for at in range(128, share, 128):
            fold = fold + sq[:, at : at + 128]
        ss[...] += fold

    def select(h):
        token = lax.broadcasted_iota(jnp.int32, (half, rows), 0) + h * half
        slot = lax.broadcasted_iota(jnp.int32, (half, rows), 1)
        at = small_ref[:, PLACE_AT : PLACE_AT + rows]
        hit = jnp.logical_and(at == token.astype(F32), slot < count_ref[0])
        return jnp.where(hit, 1.0, 0.0).astype(F32)

    def tables():
        ids = seg_ref[...].astype(F32)
        down = jnp.transpose(jnp.broadcast_to(ids, (128, tokens)))[:, 0:1]
        t = lax.broadcasted_iota(jnp.int32, (tokens, tokens), 0)
        s = lax.broadcasted_iota(jnp.int32, (tokens, tokens), 1)
        seen = jnp.where(jnp.logical_and(down == ids, s <= t), 1.0, 0.0).astype(F32)
        mask_ref[...] = seen
        position = jnp.sum(seen, axis=1, keepdims=True) - 1.0
        lane = lax.broadcasted_iota(jnp.int32, (1, HEAD_DIM), 1)
        low = lane < HEAD_DIM // 2
        order = jnp.where(low, lane, lane - HEAD_DIM // 2).astype(F32)
        angles = position * jnp.exp(order * (-2.0 * math.log(rope_base) / HEAD_DIM))
        cos, sin = jnp.cos(angles), jnp.sin(angles)
        cos_ref[...] = cos
        sin_ref[...] = jnp.where(low, -sin, sin)
        cos_t_ref[...] = jnp.transpose(cos)[0:64, :]
        sin_t_ref[...] = jnp.transpose(sin)[0:64, :]

    halves = tuple((slice(i * (half // 2), (i + 1) * (half // 2)), slice(None)) for i in range(2))

    def gather_rows(l, h):
        acc_q[h] = jnp.zeros_like(acc_q[h])
        acc_kv[h] = jnp.zeros_like(acc_kv[h])
        acc_ss[h] = jnp.zeros_like(acc_ss[h])

        def use(s):
            project(l, s, gath[h, s], acc_q.at[h], acc_kv.at[h], acc_ss.at[h])

        yield from Gather(p, gath.at[h], halves, stx.at[h], rtx.at[h]).steps(use)

    def text(h):
        if h == 0:
            for cp in loads(0):
                cp.wait()
        yield from gather_rows(0, h)
        if h == 1:
            tables()

    state = {}

    def attention(l, h):
        rows_h = slice(h * half, (h + 1) * half)
        if l == 0:
            chosen = select(h)
            image = jnp.sum(chosen, axis=1, keepdims=True) > 0.5
            exact = lax.Precision.HIGHEST
            for acc, img in ((acc_q, img_q), (acc_ss, img_ss)):
                put = jnp.dot(
                    chosen, img[0:rows, :], preferred_element_type=F32, precision=exact
                )
                acc[h] = jnp.where(image, put, acc[h])
            sides = (((1,), (1,)), ((), ()))
            put = lax.dot_general(
                img_kv[:, 0:rows], chosen, sides, preferred_element_type=F32, precision=exact
            )
            ones = jnp.ones((8, rows), F32)
            row = lax.dot_general(ones, chosen, sides, preferred_element_type=F32)[0:1, :]
            acc_kv[h] = jnp.where(row > 0.5, put, acc_kv[h])
        total = jnp.sum(acc_ss[h], axis=1, keepdims=True)
        factor = lax.rsqrt(jnp.broadcast_to(total, (half, 128)) * (1.0 / D) + rms_eps)
        factor_t = jnp.transpose(factor)
        kvx[h, p.mp] = (acc_kv[h] * factor_t[0:64, :]).astype(BF16)

        def kv_copy(i, dev):
            view = kvx.at[h, p.mp]
            return rcopy(view, view, skv.at[h, i], rkv.at[h, p.mp], dev)

        kv_to = [kv_copy(0, p.X), kv_copy(1, p.XC), kv_copy(2, p.C)]
        for cp in kv_to:
            cp.start()
        for hh in range(2):
            cols = slice(hh * 128, (hh + 1) * 128)
            q = acc_q[h, :, cols] * factor
            turned = q * cos_ref[rows_h, :] + pltpu.roll(q, 64, 1) * sin_ref[rows_h, :]
            qb[h, :, cols] = turned.astype(BF16)
        yield 2.5
        for m in (p.xo * 2 + p.c, p.xo * 2 + p.co, p.x * 2 + p.co):
            view = kvx.at[h, m]
            rcopy(view, view, skv.at[h, 0], rkv.at[h, m], p.C).wait_recv()
        state[(l, h)] = True
        assert (l, 0) in state
        keys, values = [], []
        for i in range(h + 1):
            at = slice(i * half, (i + 1) * half)
            low = jnp.concatenate([kvx[i, 0, 0:32, :], kvx[i, 1, 0:32, :]], axis=0).astype(F32)
            high = jnp.concatenate([kvx[i, 2, 0:32, :], kvx[i, 3, 0:32, :]], axis=0).astype(F32)
            cos_t, sin_t = cos_t_ref[:, at], sin_t_ref[:, at]
            keys.append(
                jnp.concatenate(
                    [low * cos_t - high * sin_t, high * cos_t + low * sin_t], axis=0
                ).astype(BF16)
            )
            values.append(jnp.concatenate([kvx[i, m, 32:64, :] for m in range(4)], axis=0))
        for hh in range(2):
            cols = slice(hh * 128, (hh + 1) * 128)
            scores = jnp.concatenate(
                [jnp.dot(qb[h, :, cols], k, preferred_element_type=F32) for k in keys], axis=1
            ) * (1.0 / math.sqrt(HEAD_DIM))
            scores = jnp.where(mask_ref[rows_h, 0 : (h + 1) * half] > 0.5, scores, -1e30)
            weights = jnp.exp(scores - jnp.max(scores, axis=-1, keepdims=True))
            weights = (weights / jnp.sum(weights, axis=-1, keepdims=True)).astype(BF16)
            out = jnp.zeros((half, HEAD_DIM), F32)
            for i, v in enumerate(values):
                out = out + lax.dot_general(
                    weights[:, i * half : (i + 1) * half],
                    v,
                    (((1,), (1,)), ((), ())),
                    preferred_element_type=F32,
                )
            attb[h, p.c, :, cols] = out.astype(BF16)
        view = attb.at[h, p.c]
        at_to = rcopy(view, view, sat.at[h], rat.at[h], p.C)
        at_to.start()
        yield 1.0
        if h == 0:
            for j in range(8):
                own_o(l, j).wait()
                give_o(l, j).wait_recv()
        view = attb.at[h, p.co]
        rcopy(view, view, sat.at[h], rat.at[h], p.C).wait_recv()

        def piece(y, x, part):
            j = y * 2 + x
            at = slice(None) if part is None else halves[part][0]
            out = jnp.dot(
                attb[h, 0, at, :], wv[l, j, 0:256, :], preferred_element_type=F32
            ) + jnp.dot(attb[h, 1, at, :], wv[l, j, 256:512, :], preferred_element_type=F32)
            return out if part is not None else [out[r, :] for r, _ in halves]

        gain = gains[min(l + 1, layers - 1), :, block(p.me)]

        def finish(part, total):
            at = slice(h * half + halves[part][0].start, h * half + halves[part][0].stop)
            new = out_ref[at, :] + total
            out_ref[at, :] = new
            if l + 1 < layers:
                gath[h, p.me, halves[part][0], :] = (new * gain).astype(BF16)

        rs = Scatter(p, sb.at[h], rb.at[h], halves, sls.at[h], rls.at[h], piece)
        yield from rs.steps(finish)
        for cp in kv_to:
            cp.wait_send()
        at_to.wait_send()

    def layer_stream(h):
        for l in range(layers):
            if l > 0:
                if h == 0:
                    for cp in loads(l):
                        cp.wait()
                yield from gather_rows(l, h)
            yield from attention(l, h)

    def weights():
        yield 0.1
        for l in range(layers):
            if l > 0:
                for cp in loads(l):
                    cp.start()
            for j in range(8):
                own_o(l, j).start()
                give_o(l, j).start()
            yield 8.0

    interleave((0.0, forward()), (0.1, text(0)), (6.0, text(1)), (4.0, weights()))
    interleave((0.0, layer_stream(0)), (3.0, layer_stream(1)), (4.0, backward()))
    for l in range(layers):
        for j in range(8):
            give_o(l, j).wait_send()


def step_call(count, small, seg, gain, patches, grads, w_in, w_out, text, q_w, kv_w, o_w):
    n_dp = 8
    xw, gw, hid = w_in.shape[0], w_out.shape[1], w_in.shape[1]
    ww = ((xw // 2 + 127) // 128) * 128
    half_out = gw // 2
    tokens, share = text.shape
    half = tokens // 2
    layers = q_w.shape[0]
    dma = pltpu.SemaphoreType.DMA
    vm = pl.BlockSpec(memory_space=pltpu.VMEM)
    hbm = pl.BlockSpec(memory_space=pl.ANY)
    V = pltpu.VMEM
    scratch = [
        V(patches.shape, BF16),
        V(grads.shape, BF16),
        V(w_in.shape, BF16),
        V(w_out.shape, BF16),
        V(text.shape, BF16),
        dma((5,)),
        V((PAD, patches.shape[1]), BF16),
        V((PAD, grads.shape[1]), BF16),
        V((n_dp, PAD, xw), BF16),
        V((n_dp, PAD, gw), BF16),
        V((2, n_dp, PAD, hid), BF16),
        V((2, n_dp, PAD, hid), BF16),
        V((2, n_dp, PAD, hid), BF16),
        V((PAD, hid), F32),
        V((n_dp, PAD, half_out), BF16),
        V((n_dp, PAD, half_out), BF16),
        V((n_dp, PAD, half_out), F32),
        V((7, PAD, half_out), BF16),
        V((7, PAD, half_out), BF16),
        V((n_dp, PAD, ww), BF16),
        V((n_dp, PAD, ww), BF16),
        V((n_dp, PAD, ww), F32),
        V((7, PAD, ww), BF16),
        V((7, PAD, ww), BF16),
        V((PAD, half_out), BF16),
        V((PAD, half_out), BF16),
        V((PAD, ww), BF16),
        V((PAD, ww), BF16),
        V((16, PAD, ww), BF16),
        V((16, PAD, share), BF16),
        V((2, 16, half, share), BF16),
        V(q_w.shape, BF16),
        V(kv_w.shape, BF16),
        V((layers, 8, 512, share), BF16),
        V((layers, 1, D), F32),
        V((layers, 1, D), F32),
        V((tokens, tokens), F32),
        V((tokens, 128), F32),
        V((tokens, 128), F32),
        V((64, tokens), F32),
        V((64, tokens), F32),
        V((2, half, 256), F32),
        V((2, 64, half), F32),
        V((2, half, 128), F32),
        V((PAD, 256), F32),
        V((64, PAD), F32),
        V((PAD, 128), F32),
        V((2, half, 256), BF16),
        V((2, 4, 64, half), BF16),
        V((2, 2, half, 256), BF16),
        V((2, 7, half, share), BF16),
        V((2, 7, half, share), BF16),
        dma((2, n_dp)),
        dma((2, n_dp)),
        dma((2, n_dp)),
        dma((2, n_dp)),
        dma((2, n_dp)),
        dma((2, n_dp)),
        dma((2, n_dp)),
        dma((2,)),
        dma((2,)),
        dma((2, 14)),
        dma((2, 14)),
        dma((2,)),
        dma((2,)),
        dma((GATHER_SENDS,)),
        dma((32,)),
        dma((GATHER_SENDS,)),
        dma((32,)),
        dma((layers,)),
        dma((layers, 2)),
        dma((layers, 8)),
        dma((layers, 8)),
        dma((layers, 8)),
        dma((2, GATHER_SENDS)),
        dma((2, 32)),
        dma((2, 3)),
        dma((2, 4)),
        dma((2,)),
        dma((2,)),
        dma((2, 14)),
        dma((2, 14)),
    ]
    return pl.pallas_call(
        step_kernel,
        out_shape=(
            jax.ShapeDtypeStruct(text.shape, F32),
            jax.ShapeDtypeStruct(patches.shape, F32),
        ),
        in_specs=[pl.BlockSpec(memory_space=pltpu.SMEM)] + [vm] * 3 + [hbm] * 8,
        out_specs=(vm, vm),
        scratch_shapes=scratch,
        compiler_params=pltpu.CompilerParams(
            collective_id=0, has_side_effects=True, vmem_limit_bytes=58 * 2**20
        ),
    )(count, small, seg, gain, patches, grads, w_in, w_out, text, q_w, kv_w, o_w)


def local(
    patches,
    ln_gain,
    ln_shift,
    w_in,
    b_in,
    w_out,
    b_out,
    place,
    image_counts,
    text_rows,
    segments,
    norm_gain,
    q_weight,
    kv_weight,
    o_weight,
    grad_rows,
):
    spots = jnp.pad(place.astype(F32), (0, 128 - place.shape[0]))
    small = jnp.concatenate(
        [x.astype(F32) for x in (ln_gain, ln_shift, b_out)] + [spots, b_in.astype(F32)]
    )[None]
    return step_call(
        image_counts,
        small,
        segments,
        norm_gain,
        patches,
        grad_rows,
        w_in,
        w_out,
        text_rows,
        q_weight,
        kv_weight,
        o_weight,
    )


def solution(mesh):
    in_specs = (
        P("dp", None),
        P(),
        P(),
        P("dp", ("sec", "mp")),
        P(("sec", "mp")),
        P(("sec", "mp"), "dp"),
        P(("sec", "mp")),
        P("dp"),
        P("dp"),
        P("dp", ("sec", "mp")),
        P("dp", None),
        P(),
        P(None, None, ("sec", "mp")),
        P(None, None, ("sec", "mp"), None),
        P(None, ("sec", "mp"), None),
        P("dp", None),
    )
    out_specs = (P("dp", ("sec", "mp")), P("dp", None))
    return jax.shard_map(local, mesh=mesh, in_specs=in_specs, out_specs=out_specs, check_vma=False)
```
